128 devices in a mesh: dp: 32 (over z, y, x_lo), tensor: 4 (over x_hi, core).
Axes of the slice: x: 4 (x_hi: 2, x_lo: 2; x = x_hi * 2 + x_lo), y: 4, z: 4, core: 2. Of those that a mesh axis runs over, the one named last changes fastest.
Arguments:
- hidden_in: float32 [4096, 1024], P('dp'), may hold values from -6 to 6
- cotangent: float32 [4096, 1024], P('dp'), may hold values from -6 to 6
- seq_lengths: int32 [32, 4], P('dp'), may hold values from 1 to 64, 128 in all within a row
- routes: int32 [2, 4096, 8], P(None, 'dp'), may hold values from 0 to 31, all different within a row; in each aligned block of 128 rows (0 to 127, 128 to 255, ..., all dimensions but the last counted through in order) at most 48 rows name the same one
- norm_attn: float32 [2, 1024], replicated, may hold values from 0.25 to 1.75
- norm_moe: float32 [2, 1024], replicated, may hold values from 0.25 to 1.75
- w_query: bfloat16 [2, 1024, 1024], P(None, None, 'tensor'), may hold values from -0.1875 to 0.1875
- w_key: bfloat16 [2, 1024, 512], P(None, None, 'tensor'), may hold values from -0.1875 to 0.1875
- w_value: bfloat16 [2, 1024, 512], P(None, None, 'tensor'), may hold values from -0.1875 to 0.1875
- w_output: bfloat16 [2, 1024, 1024], P(None, 'tensor'), may hold values from -0.75 to 0.75
- w_router: bfloat16 [2, 1024, 32], replicated, may hold values from -0.375 to 0.375
- w_gate: bfloat16 [2, 32, 1024, 512], P(None, 'dp', None, 'tensor'), may hold values from -0.1875 to 0.1875
- w_up: bfloat16 [2, 32, 1024, 512], P(None, 'dp', None, 'tensor'), may hold values from -0.1875 to 0.1875
- w_down: bfloat16 [2, 32, 512, 1024], P(None, 'dp', 'tensor'), may hold values from -0.375 to 0.375
Outputs:
- output: float32 [4096, 1024], P('dp')
- d_hidden_in: float32 [4096, 1024], P('dp')
- d_norm_attn: float32 [2, 1024], P(None, 'dp')
- d_norm_moe: float32 [2, 1024], P(None, 'dp')
- d_w_query: float32 [2, 1024, 1024], P(None, 'dp', 'tensor')
- d_w_key: float32 [2, 1024, 512], P(None, 'dp', 'tensor')
- d_w_value: float32 [2, 1024, 512], P(None, 'dp', 'tensor')
- d_w_output: float32 [2, 1024, 1024], P(None, 'tensor', 'dp')
- d_w_router: float32 [2, 1024, 32], P(None, 'dp')
- d_w_gate: float32 [2, 32, 1024, 512], P(None, 'dp', None, 'tensor')
- d_w_up: float32 [2, 32, 1024, 512], P(None, 'dp', None, 'tensor')
- d_w_down: float32 [2, 32, 512, 1024], P(None, 'dp', 'tensor')
The draws below stay inside these ranges and needn't reach their ends.
Inputs may be any that keep to these rules, and one draw needn't show every extreme that they name: `seq_lengths`: each row sums to 128 and its largest entry is 64. `routes`: each token names 8 different experts in each layer; among the 128 tokens of one index of dp no expert is named more than 48 times in a layer, a bound that some block reaches there.
All inputs are finite; a program needn't handle non-finite values.
Results may differ from the reference program's by a relative error of at most 0.03.
Values may be sent and summed in bfloat16 or wider, within the bound.
No kernel may reach another device: no remote copies, remote signals or barrier semaphores. Data moves between devices by JAX's collectives and lax.ppermute only.
A program may use at most 128 MiB of HBM per device.

```python
import math
import jax
import jax.numpy as jnp
import numpy as np
from jax import lax

D = 1024
H = 16
KV = 8
HD = 64
E = 32
FF = 512
TOPK = 8
LAYERS = 2
NSEQ = 4
TOK_DEV = 128
CAP = 48
LMAX = 64
TOKENS = 4096
N_DP = 32


def block_scale(key, shape, cuts, low, high):
    loudness, own = 1.0, jax.random.fold_in(key, 6)
    for dim, blocks in cuts:
        heights = jnp.exp(jax.random.uniform(jax.random.fold_in(own, dim), (blocks,), jnp.float32, low / len(cuts), high / len(cuts)))
        loudness = loudness * jnp.repeat(heights, shape[dim] // blocks).reshape([-1 if axis == dim else 1 for axis in range(len(shape))])
    return loudness


def length_profile(number_of, total, bound, skew):
    portions = [(1 << 20) // math.isqrt(grade ** skew) + 1 for grade in range(2, number_of + 1)]
    spare, given = total - bound - (number_of - 1), [1] * (number_of - 1)
    while spare > 0:
        free = [i for i in range(number_of - 1) if given[i] < bound]
        pool, left = sum([portions[i] for i in free]), spare
        for i in free:
            more = min(bound - given[i], max(1, left * portions[i] // pool), spare)
            given[i] = given[i] + more
            spare = spare - more
    return np.array([bound] + given)


def uneven_parts(rng, number_of, total, limit, lean):
    if number_of == 2:
        one = jax.random.randint(rng, (), max(1, total - limit), min(limit, total - 1) + 1)
        return jnp.stack([one, total - one])
    sizes = jnp.asarray(length_profile(number_of, total, limit, lean), jnp.int32)
    couples = (number_of - 1) // 2
    giver, sink = sizes[1:1 + 2 * couples:2], sizes[2:2 + 2 * couples:2]
    room = jnp.minimum(giver - 1, limit - sink)
    passed = jax.random.randint(jax.random.fold_in(rng, 1), (couples,), 0, 1 << 20) % (room + 1)
    sizes = sizes.at[1:1 + 2 * couples:2].set(giver - passed).at[2:2 + 2 * couples:2].set(sink + passed)
    return sizes[jax.random.permutation(jax.random.fold_in(rng, 2), number_of)]


def routed_block(stream_key, own, number, rows, number_of, top, reach, lean):
    sequence = jax.random.permutation(stream_key, number_of)
    heavy_load, usual = shares(number_of, rows * top, reach, lean, True), shares(number_of, rows * top, reach, lean, False)
    places = jnp.arange(number_of)

    def named(sizes, turn):
        used = int((sizes > 0).sum())
        fixed = max(1, used // 4)
        shifted = fixed + (places - fixed + turn * (used - fixed)) % max(1, number_of - fixed)
        return jnp.zeros((number_of,), jnp.int32).at[sequence[jnp.where(places < fixed, places, shifted)]].set(jnp.asarray(sizes, jnp.int32))

    sizes = jnp.where(number % 4 == 0, named(heavy_load, number // 4), named(usual, number - number // 4 - 1))
    mixed = jax.random.permutation(jax.random.fold_in(own, 3), number_of)
    source_of, sink = mixed[0:number_of // 2 * 2:2], mixed[1:number_of // 2 * 2:2]
    room = jnp.minimum(sizes[source_of] - 1, reach - sizes[sink]) // 2
    room = jnp.where((source_of == sequence[0]) | (sink == sequence[0]) | (sizes[sink] == 0), 0, jnp.maximum(room, 0))
    shifted = jax.random.randint(jax.random.fold_in(own, 4), (number_of // 2,), 0, 1 << 20) % (room + 1)
    sizes = sizes.at[source_of].add(-shifted).at[sink].add(shifted)
    items = jnp.searchsorted(jnp.cumsum(sizes), jnp.arange(rows * top), side="right").astype(jnp.int32)
    table = items.reshape(top, rows).T
    table = table[jax.random.permutation(jax.random.fold_in(own, 1), rows)]
    turn = jax.random.randint(jax.random.fold_in(own, 2), (rows, 1), 0, top)
    return jnp.take_along_axis(table, (jnp.arange(top)[None, :] + turn) % top, axis=1)


def shares(count, total, limit, slope, full):
    portions = [(1 << 20) // math.isqrt(rank ** slope) + 1 for rank in range(1, count + 1)]
    largest = limit if full else min(limit, max(-(-total // count), total * portions[0] // sum(portions)))
    least = 1 if total - largest >= count - 1 else 0
    counts, surplus = [largest] + [least] * (count - 1), total - largest - least * (count - 1)
    while surplus > 0:
        movable = [i for i in range(1, count) if counts[i] < largest] or [i for i in range(1, count) if counts[i] < limit]
        mass, remaining = sum([portions[i] for i in movable]), surplus
        for i in movable:
            extra = min(limit - counts[i], max(1, remaining * portions[i] // mass), surplus)
            counts[i] = counts[i] + extra
            surplus = surplus - extra
    return np.array(counts)


def centred(key, dims, width, bound, pieces=(), held_as=jnp.bfloat16):
    level = block_scale(key, dims, pieces, -0.22, 0.18) if pieces else 1.0
    array = jax.random.normal(key, dims, jnp.float32) * width * level
    return jnp.minimum(jnp.maximum(array, -bound), bound).astype(held_as)


def setup_inputs(seed: int = 0) -> dict:
    key_list = jax.random.split(jax.random.key(seed), 15)
    hidden_in = centred(key_list[0], (TOKENS, D), 1.0, 6.0, ((0, 32),), jnp.float32)
    cotangent = centred(key_list[1], (TOKENS, D), 1.0, 6.0, ((0, 32),), jnp.float32)
    seq_lengths = jax.vmap(lambda own: uneven_parts(own, NSEQ, TOK_DEV, LMAX, 2))(jax.random.split(key_list[2], N_DP)).reshape((N_DP, NSEQ)).astype(jnp.int32)
    routes_keys = jax.random.split(jax.random.fold_in(key_list[3], 1), LAYERS * TOKENS // TOK_DEV)
    routes_turns = jax.random.permutation(jax.random.fold_in(key_list[3], 3), LAYERS * TOKENS // TOK_DEV)
    routes = jax.vmap(lambda own, number: routed_block(jax.random.fold_in(key_list[3], 2), own, number, TOK_DEV, E, TOPK, CAP, 2))(routes_keys, routes_turns).reshape((LAYERS, TOKENS, TOPK))
    norm_attn = jnp.clip(1.0 + 0.15 * jax.random.normal(key_list[4], (LAYERS, D), jnp.float32), 0.25, 1.75)
    norm_moe = jnp.clip(1.0 + 0.15 * jax.random.normal(key_list[5], (LAYERS, D), jnp.float32), 0.25, 1.75)
    w_query = centred(key_list[6], (LAYERS, D, H * HD), D ** -0.5, 0.1875, ((2, 4),))
    w_key = centred(key_list[7], (LAYERS, D, KV * HD), D ** -0.5, 0.1875, ((2, 4),))
    w_value = centred(key_list[8], (LAYERS, D, KV * HD), D ** -0.5, 0.1875, ((2, 4),))
    w_output = centred(key_list[9], (LAYERS, H * HD, D), HD ** -0.5, 0.75, ((1, 4),))
    w_router = centred(key_list[10], (LAYERS, D, E), (D // 4) ** -0.5, 0.375)
    w_gate = centred(key_list[11], (LAYERS, E, D, FF), D ** -0.5, 0.1875, ((1, 32), (3, 4)))
    w_up = centred(key_list[12], (LAYERS, E, D, FF), D ** -0.5, 0.1875, ((1, 32), (3, 4)))
    w_down = centred(key_list[13], (LAYERS, E, FF, D), (FF // 2) ** -0.5, 0.375, ((1, 32), (2, 4)))
    return dict(hidden_in=hidden_in, cotangent=cotangent, seq_lengths=seq_lengths, routes=routes, norm_attn=norm_attn, norm_moe=norm_moe, w_query=w_query, w_key=w_key, w_value=w_value, w_output=w_output, w_router=w_router, w_gate=w_gate, w_up=w_up, w_down=w_down)


EPS = 1e-05
SCALE = 0.125
NEGATIVE = -1e+30

def norm_forward(hidden, gain):
    inverse_root = lax.rsqrt(lax.optimization_barrier(jnp.mean(hidden * hidden, axis=-1, keepdims=True)) + EPS)
    return (hidden * inverse_root * gain, inverse_root)

def norm_backward(hidden, inverse_root, gain, d_normed):
    scaled = gain * d_normed
    d_hidden = inverse_root * (scaled - hidden * inverse_root * inverse_root * lax.optimization_barrier(jnp.mean(scaled * hidden, axis=-1, keepdims=True)))
    d_gain = lax.optimization_barrier(jnp.sum(d_normed * hidden * inverse_root, axis=0))
    return (d_hidden, d_gain)

def rope_tables(lengths, count):
    ends = jnp.cumsum(lengths).astype(jnp.int32)
    starts = ends - lengths
    index = jnp.arange(count, dtype=jnp.int32)
    segment = lax.optimization_barrier(jnp.sum((index[:, None] >= ends[None, :]).astype(jnp.int32), axis=1))
    member = segment[:, None] == jnp.arange(lengths.shape[0], dtype=jnp.int32)[None, :]
    begin = lax.optimization_barrier(jnp.sum(jnp.where(member, starts[None, :], 0), axis=1))
    position = (index - begin).astype(jnp.float32)
    half = HD // 2
    inverse = jnp.exp(-jnp.log(10000.0) * jnp.arange(half, dtype=jnp.float32) * 2.0 / HD)
    angle = position[:, None] * inverse[None, :]
    allowed = (segment[:, None] == segment[None, :]) & (index[None, :] <= index[:, None])
    return (jnp.cos(angle), jnp.sin(angle), allowed)

def rotate(values, cosine, sine):
    half = values.shape[-1] // 2
    first, second = (values[..., :half], values[..., half:])
    cos_rows, sin_rows = (cosine[:, None, :], sine[:, None, :])
    return jnp.concatenate([first * cos_rows - second * sin_rows, second * cos_rows + first * sin_rows], axis=-1)

def unrotate(values, cosine, sine):
    half = values.shape[-1] // 2
    first, second = (values[..., :half], values[..., half:])
    cos_rows, sin_rows = (cosine[:, None, :], sine[:, None, :])
    return jnp.concatenate([first * cos_rows + second * sin_rows, second * cos_rows - first * sin_rows], axis=-1)

def slots_for(routing):
    count, top = routing.shape
    onehot = (routing[:, :, None] == jnp.arange(E, dtype=jnp.int32)[None, None, :]).astype(jnp.int32)
    per_token = lax.optimization_barrier(jnp.sum(onehot, axis=1))
    before = jnp.cumsum(per_token, axis=0).astype(jnp.int32) - per_token
    rank = lax.optimization_barrier(jnp.sum(onehot * before[:, None, :], axis=2))
    slot = (routing * CAP + rank).astype(jnp.int32)
    pair = jnp.full((E * CAP,), count * top, jnp.int32).at[slot.reshape(-1)].set(jnp.arange(count * top, dtype=jnp.int32))
    token = (pair // top).astype(jnp.int32)
    return (onehot, slot, pair, token)

def project_heads(normed_b, weight, cosine, sine, turn):
    raw = jnp.dot(normed_b, weight, preferred_element_type=jnp.float32)
    shaped = raw.reshape(raw.shape[0], -1, HD)
    if turn:
        shaped = rotate(shaped, cosine, sine)
    return shaped.astype(jnp.bfloat16)

def attend(query, keys, values, allowed):
    count, kv_heads, size = keys.shape
    group = query.shape[1] // kv_heads
    grouped = query.reshape(count, kv_heads, group, size).astype(jnp.float32)
    scores = jnp.einsum('qkgd,tkd->kgqt', grouped, keys.astype(jnp.float32)) * SCALE
    scores = jnp.where(allowed[None, None], scores, NEGATIVE)
    top = lax.optimization_barrier(jnp.max(scores, axis=-1, keepdims=True))
    expd = jnp.exp(scores - top)
    total = lax.optimization_barrier(jnp.sum(expd, axis=-1, keepdims=True))
    lse = top + jnp.log(total)
    probs = (expd / total).astype(jnp.bfloat16)
    mixed = jnp.einsum('kgqt,tkd->qkgd', probs.astype(jnp.float32), values.astype(jnp.float32))
    return (mixed.reshape(count, -1).astype(jnp.bfloat16), lse)

def attend_back(query, keys, values, lse, allowed, d_mixed):
    count, kv_heads, size = keys.shape
    group = query.shape[1] // kv_heads
    grouped = query.reshape(count, kv_heads, group, size).astype(jnp.float32)
    keys_f = keys.astype(jnp.float32)
    scores = jnp.einsum('qkgd,tkd->kgqt', grouped, keys_f) * SCALE
    probs = jnp.where(allowed[None, None], jnp.exp(scores - lse), 0.0)
    probs_b = probs.astype(jnp.bfloat16).astype(jnp.float32)
    d_grouped = d_mixed.reshape(count, kv_heads, group, size).astype(jnp.float32)
    d_values = jnp.einsum('kgqt,qkgd->tkd', probs_b, d_grouped)
    d_probs = jnp.einsum('qkgd,tkd->kgqt', d_grouped, values.astype(jnp.float32))
    delta = lax.optimization_barrier(jnp.sum(probs * d_probs, axis=-1, keepdims=True))
    d_scores = (probs * (d_probs - delta) * SCALE).astype(jnp.bfloat16).astype(jnp.float32)
    d_query = jnp.einsum('kgqt,tkd->qkgd', d_scores, keys_f).reshape(count, -1, size)
    d_keys = jnp.einsum('kgqt,qkgd->tkd', d_scores, grouped)
    return (d_query, d_keys, d_values)

def front(hidden, lengths, routing, weights):
    gain_one, gain_two, wq, wk, wv, wo, wr = weights
    count = hidden.shape[0]
    cosine, sine, allowed = rope_tables(lengths, count)
    normed, inverse_one = norm_forward(hidden, gain_one)
    normed_b = normed.astype(jnp.bfloat16)
    query = project_heads(normed_b, wq, cosine, sine, True)
    keys = project_heads(normed_b, wk, cosine, sine, True)
    values = project_heads(normed_b, wv, cosine, sine, False)
    mixed, lse = attend(query, keys, values, allowed)
    middle = hidden + jnp.dot(mixed, wo, preferred_element_type=jnp.float32)
    normed_two, inverse_two = norm_forward(middle, gain_two)
    moe_in = normed_two.astype(jnp.bfloat16)
    logits = jnp.dot(moe_in, wr, preferred_element_type=jnp.float32)
    onehot, slot, pair, token = slots_for(routing)
    chosen = lax.optimization_barrier(jnp.sum(jnp.where(onehot > 0, logits[:, None, :], 0.0), axis=2))
    gates = jax.nn.softmax(chosen, axis=-1)
    padded = jnp.concatenate([moe_in, jnp.zeros((1, moe_in.shape[1]), jnp.bfloat16)], axis=0)
    send = padded[token]
    return (middle, normed_b, inverse_one, query, keys, values, mixed, lse, moe_in, inverse_two, gates, onehot, slot, pair, send)

def owner_view(rows):
    return rows.reshape(N_DP, E, CAP, D).transpose(1, 0, 2, 3).reshape(E, N_DP * CAP, D)

def source_view(rows):
    return rows.reshape(E, N_DP, CAP, D).transpose(1, 0, 2, 3).reshape(N_DP, E * CAP, D)

def expert_forward(rows, w_gate, w_up, w_down):

    def one(items):
        inputs, gate_w, up_w, down_w = items
        gate = jnp.dot(inputs, gate_w, preferred_element_type=jnp.float32)
        upper = jnp.dot(inputs, up_w, preferred_element_type=jnp.float32)
        act = (gate * jax.nn.sigmoid(gate) * upper).astype(jnp.bfloat16)
        return jnp.dot(act, down_w, preferred_element_type=jnp.float32).astype(jnp.bfloat16)
    return lax.map(one, (rows, w_gate, w_up, w_down))

def expert_backward(rows, d_rows, w_gate, w_up, w_down):

    def one(items):
        inputs, d_out, gate_w, up_w, down_w = items
        gate = jnp.dot(inputs, gate_w, preferred_element_type=jnp.float32)
        upper = jnp.dot(inputs, up_w, preferred_element_type=jnp.float32)
        sig = jax.nn.sigmoid(gate)
        act = (gate * sig * upper).astype(jnp.bfloat16)
        d_act = jnp.dot(d_out, down_w.T, preferred_element_type=jnp.float32)
        d_down = jnp.dot(act.T, d_out, preferred_element_type=jnp.float32)
        d_upper = (d_act * gate * sig).astype(jnp.bfloat16)
        d_gate = (d_act * upper * sig * (1.0 + gate * (1.0 - sig))).astype(jnp.bfloat16)
        d_gate_w = jnp.dot(inputs.T, d_gate, preferred_element_type=jnp.float32)
        d_up_w = jnp.dot(inputs.T, d_upper, preferred_element_type=jnp.float32)
        d_inputs = jnp.dot(d_gate, gate_w.T, preferred_element_type=jnp.float32) + jnp.dot(d_upper, up_w.T, preferred_element_type=jnp.float32)
        return (d_inputs.astype(jnp.bfloat16), d_gate_w, d_up_w, d_down)
    return lax.map(one, (rows, d_rows, w_gate, w_up, w_down))

def moe_back(d_hidden, gates, onehot, pair, picked):
    d_gates = lax.optimization_barrier(jnp.sum(picked * d_hidden[:, None, :], axis=-1))
    d_chosen = gates * (d_gates - lax.optimization_barrier(jnp.sum(gates * d_gates, axis=-1, keepdims=True)))
    d_logits = lax.optimization_barrier(jnp.sum(onehot.astype(jnp.float32) * d_chosen[:, :, None], axis=1))
    d_picked = (gates[:, :, None] * d_hidden[:, None, :]).astype(jnp.bfloat16)
    flat = d_picked.reshape(-1, d_picked.shape[2])
    padded = jnp.concatenate([flat, jnp.zeros((1, flat.shape[1]), jnp.bfloat16)], axis=0)
    return (padded[pair], d_logits)

def rest_back(layer_input, lengths, d_hidden, d_rows, d_logits, saved, weights):
    gain_one, gain_two, wq, wk, wv, wo, wr = weights
    middle, normed_b, inverse_one, query, keys, values, mixed, lse, moe_in, inverse_two, gates, onehot, slot, pair, send = saved
    count = layer_input.shape[0]
    cosine, sine, allowed = rope_tables(lengths, count)
    router_f = wr.astype(jnp.float32)
    d_normed_two = lax.optimization_barrier(jnp.sum(d_rows[slot], axis=1, dtype=jnp.float32)) + jnp.dot(d_logits, router_f.T, precision=lax.Precision.HIGHEST)
    d_router = jnp.dot(moe_in.astype(jnp.float32).T, d_logits, precision=lax.Precision.HIGHEST)
    d_mid_norm, d_gain_two = norm_backward(middle, inverse_two, gain_two, d_normed_two)
    d_middle = d_hidden + d_mid_norm
    d_middle_b = d_middle.astype(jnp.bfloat16)
    d_output_w = jnp.dot(mixed.T, d_middle_b, preferred_element_type=jnp.float32)
    d_mixed = jnp.dot(d_middle_b, wo.T, preferred_element_type=jnp.float32).astype(jnp.bfloat16)
    d_query, d_keys, d_values = attend_back(query, keys, values, lse, allowed, d_mixed)
    d_query = unrotate(d_query, cosine, sine).reshape(count, -1).astype(jnp.bfloat16)
    d_keys = unrotate(d_keys, cosine, sine).reshape(count, -1).astype(jnp.bfloat16)
    d_values = d_values.reshape(count, -1).astype(jnp.bfloat16)
    d_query_w = jnp.dot(normed_b.T, d_query, preferred_element_type=jnp.float32)
    d_key_w = jnp.dot(normed_b.T, d_keys, preferred_element_type=jnp.float32)
    d_value_w = jnp.dot(normed_b.T, d_values, preferred_element_type=jnp.float32)
    d_normed_one = jnp.dot(d_query, wq.T, preferred_element_type=jnp.float32) + jnp.dot(d_keys, wk.T, preferred_element_type=jnp.float32) + jnp.dot(d_values, wv.T, preferred_element_type=jnp.float32)
    d_hid_norm, d_gain_one = norm_backward(layer_input, inverse_one, gain_one, d_normed_one)
    return (d_middle + d_hid_norm, (d_query_w, d_key_w, d_value_w, d_output_w, d_gain_one, d_gain_two, d_router))

def reference(hidden_in, cotangent, seq_lengths, routes, norm_attn, norm_moe, w_query, w_key, w_value, w_output, w_router, w_gate, w_up, w_down):
    hidden = hidden_in.reshape(N_DP, TOK_DEV, D)
    route_blocks = routes.reshape(LAYERS, N_DP, TOK_DEV, TOPK)
    kept = []
    for layer in range(LAYERS):
        weights = (norm_attn[layer], norm_moe[layer], w_query[layer], w_key[layer], w_value[layer], w_output[layer], w_router[layer])
        saved = lax.map(lambda block: front(block[0], block[1], block[2], weights), (hidden, seq_lengths, route_blocks[layer]))
        returned = source_view(expert_forward(owner_view(saved[14]), w_gate[layer], w_up[layer], w_down[layer]))
        picked = jax.vmap(lambda rows, slot: rows[slot])(returned, saved[12])
        hidden_next = saved[0] + lax.optimization_barrier(jnp.sum(saved[10][..., None] * picked, axis=2))
        kept.append((hidden, saved, picked))
        hidden = hidden_next
    output = hidden.reshape(TOKENS, D)
    d_hidden = cotangent.reshape(N_DP, TOK_DEV, D)
    grads = [None] * LAYERS
    experts = [None] * LAYERS
    for layer in reversed(range(LAYERS)):
        weights = (norm_attn[layer], norm_moe[layer], w_query[layer], w_key[layer], w_value[layer], w_output[layer], w_router[layer])
        layer_input, saved, picked = kept[layer]
        d_send, d_logits = jax.vmap(moe_back)(d_hidden, saved[10], saved[11], saved[13], picked)
        d_inputs, d_gate_w, d_up_w, d_down_w = expert_backward(owner_view(saved[14]), owner_view(d_send), w_gate[layer], w_up[layer], w_down[layer])
        d_rows = source_view(d_inputs)
        d_hidden, block_grads = lax.map(lambda block: rest_back(block[0], block[1], block[2], block[3], block[4], block[5], weights), (layer_input, seq_lengths, d_hidden, d_rows, d_logits, saved))
        grads[layer] = tuple((lax.optimization_barrier(jnp.sum(item, axis=0)) for item in block_grads))
        experts[layer] = (d_gate_w, d_up_w, d_down_w)
    stacked = [jnp.stack([grads[layer][item] for layer in range(LAYERS)]) for item in range(7)]
    expert_stack = [jnp.stack([experts[layer][item] for layer in range(LAYERS)]) for item in range(3)]
    return (output, d_hidden.reshape(TOKENS, D), stacked[4], stacked[5], stacked[0], stacked[1], stacked[2], stacked[3], stacked[6], expert_stack[0], expert_stack[1], expert_stack[2])
```

```python
import functools
import jax
import jax.numpy as jnp
from jax import lax
from jax.experimental import pallas as pl
from jax.experimental.pallas import tpu as pltpu
from jax.sharding import PartitionSpec as P

HD = 64
E = 32
WAYS = 4
ROOM = 16
EPS = 1e-05
SCALE = 0.125
NEGATIVE = -1e30
F32 = jnp.float32
BF16 = jnp.bfloat16


def dot(a, b, ca=1, cb=0, precision=None):
    return lax.dot_general(
        a, b, (((ca,), (cb,)), ((), ())), preferred_element_type=F32, precision=precision
    )


def norm_forward(hidden, gain):
    inverse_root = lax.rsqrt(jnp.mean(hidden * hidden, axis=-1, keepdims=True) + EPS)
    return (hidden * inverse_root * gain, inverse_root)


def norm_backward(hidden, inverse_root, gain, d_normed):
    scaled = gain * d_normed
    d_hidden = inverse_root * (
        scaled
        - hidden * inverse_root * inverse_root * jnp.mean(scaled * hidden, axis=-1, keepdims=True)
    )
    d_gain = jnp.sum(d_normed * hidden * inverse_root, axis=0)
    return (d_hidden, d_gain)


def rope_tables(lengths, count):
    ends = jnp.cumsum(lengths)
    starts = ends - lengths
    index = jnp.arange(count, dtype=jnp.int32)
    segment = jnp.sum((index[:, None] >= ends[None, :]).astype(jnp.int32), axis=1)
    member = segment[:, None] == jnp.arange(lengths.shape[0], dtype=jnp.int32)[None, :]
    begin = jnp.sum(jnp.where(member, starts[None, :], 0), axis=1)
    position = (index - begin).astype(F32)
    half = HD // 2
    inverse = jnp.exp(-jnp.log(10000.0) * jnp.arange(half, dtype=F32) * 2.0 / HD)
    angle = position[:, None] * inverse[None, :]
    allowed = (segment[:, None] == segment[None, :]) & (index[None, :] <= index[:, None])
    return (jnp.cos(angle), jnp.sin(angle), allowed)


def rotate(values, cosine, sine):
    half = values.shape[-1] // 2
    first, second = (values[..., :half], values[..., half:])
    cos_rows, sin_rows = (cosine[:, None, :], sine[:, None, :])
    return jnp.concatenate(
        [first * cos_rows - second * sin_rows, second * cos_rows + first * sin_rows], axis=-1
    )


def unrotate(values, cosine, sine):
    return rotate(values, cosine, -sine)


def project_heads(normed_b, weight, cosine, sine, turn):
    raw = dot(normed_b, weight)
    shaped = raw.reshape(raw.shape[0], -1, HD)
    if turn:
        shaped = rotate(shaped, cosine, sine)
    return shaped.astype(BF16)


def attend(query, keys, values, allowed):
    count, kv_heads, size = keys.shape
    group = query.shape[1] // kv_heads
    grouped = query.reshape(count, kv_heads, group, size)
    scores = jnp.einsum("qkgd,tkd->kgqt", grouped, keys, preferred_element_type=F32) * SCALE
    scores = jnp.where(allowed[None, None], scores, NEGATIVE)
    top = jnp.max(scores, axis=-1, keepdims=True)
    expd = jnp.exp(scores - top)
    total = jnp.sum(expd, axis=-1, keepdims=True)
    lse = top + jnp.log(total)
    probs = (expd / total).astype(BF16)
    mixed = jnp.einsum("kgqt,tkd->qkgd", probs, values, preferred_element_type=F32)
    return (mixed.reshape(count, -1).astype(BF16), lse)


def attend_back(query, keys, values, lse, allowed, d_mixed):
    count, kv_heads, size = keys.shape
    group = query.shape[1] // kv_heads
    grouped = query.reshape(count, kv_heads, group, size)
    scores = jnp.einsum("qkgd,tkd->kgqt", grouped, keys, preferred_element_type=F32) * SCALE
    probs = jnp.where(allowed[None, None], jnp.exp(scores - lse), 0.0)
    probs_b = probs.astype(BF16)
    d_grouped = d_mixed.reshape(count, kv_heads, group, size)
    d_values = jnp.einsum("kgqt,qkgd->tkd", probs_b, d_grouped, preferred_element_type=F32)
    d_probs = jnp.einsum("qkgd,tkd->kgqt", d_grouped, values, preferred_element_type=F32)
    delta = jnp.sum(probs * d_probs, axis=-1, keepdims=True)
    d_scores = (probs * (d_probs - delta) * SCALE).astype(BF16)
    d_query = jnp.einsum("kgqt,tkd->qkgd", d_scores, keys, preferred_element_type=F32)
    d_keys = jnp.einsum("kgqt,qkgd->tkd", d_scores, grouped, preferred_element_type=F32)
    return (d_query.reshape(count, -1, size), d_keys, d_values)


def swap(value, mask):
    return lax.ppermute(value, "tensor", [(i, i ^ mask) for i in range(WAYS)])


def tensor_total(part):
    mine = lax.optimization_barrier(part.astype(BF16))
    pair = lax.optimization_barrier((mine.astype(F32) + swap(mine, 1).astype(F32)).astype(BF16))
    return pair.astype(F32) + swap(pair, 2).astype(F32)


def exchange(rows):
    return lax.all_to_all(rows, "dp", split_axis=0, concat_axis=0, tiled=True)


def dp_total(part):
    arrived = exchange(part.astype(BF16))
    return jnp.sum(arrived.reshape(E, -1, part.shape[1]).astype(F32), axis=0)


def expert_kernel(want_out, want_back, *refs):
    refs = list(refs)
    rows = refs.pop(0)[...]
    d_rows = refs.pop(0)[...] if want_back else None
    pairs, downs, refs = refs[:WAYS], refs[WAYS : 2 * WAYS], refs[2 * WAYS :]
    out_ref = refs.pop(0) if want_out else None
    if want_back:
        d_rows_ref = refs.pop(0)
        d_pairs, d_downs, refs = refs[:WAYS], refs[WAYS : 2 * WAYS], refs[2 * WAYS :]
    out_sum = refs.pop(0) if want_out else None
    back_sum = refs.pop(0) if want_back else None
    for block in range(WAYS):
        both = dot(rows, pairs[block][...])
        width = both.shape[1] // 2
        gate, upper = both[:, :width], both[:, width:]
        sig = jax.nn.sigmoid(gate)
        act = (gate * sig * upper).astype(BF16)
        if want_out:
            term = dot(act, downs[block][...])
            out_sum[...] = term if block == 0 else out_sum[...] + term
        if want_back:
            d_act = dot(d_rows, downs[block][...], 1, 1)
            d_downs[block][...] = dot(act, d_rows, 0, 0).astype(d_downs[block].dtype)
            d_upper = (d_act * gate * sig).astype(BF16)
            d_gate = (d_act * upper * sig * (1.0 + gate * (1.0 - sig))).astype(BF16)
            d_both = jnp.concatenate([d_gate, d_upper], axis=1)
            term = dot(d_both, pairs[block][...], 1, 1)
            back_sum[...] = term if block == 0 else back_sum[...] + term
            d_pairs[block][...] = dot(rows, d_both, 0, 0).astype(d_pairs[block].dtype)
    if want_out:
        out_ref[...] = out_sum[...].astype(BF16)
    if want_back:
        d_rows_ref[...] = back_sum[...].astype(BF16)


def experts(rows, d_rows, weights, want_out):
    pairs, downs = weights
    want_back = d_rows is not None
    args = [rows] + ([d_rows] if want_back else []) + list(pairs) + list(downs)
    like = jax.ShapeDtypeStruct(rows.shape, BF16)
    outs = [like] if want_out else []
    kinds = (F32, BF16, F32, BF16)
    if want_back:
        outs = outs + [like]
        outs = outs + [jax.ShapeDtypeStruct(w.shape, k) for w, k in zip(pairs, kinds)]
        outs = outs + [jax.ShapeDtypeStruct(w.shape, k) for w, k in zip(downs, kinds)]
    sums = [pltpu.VMEM(rows.shape, F32)] * (int(want_out) + int(want_back))
    vmem = pl.BlockSpec(memory_space=pltpu.VMEM)
    products = 2 * rows.shape[0] * rows.shape[1] * 128 * WAYS
    return pl.pallas_call(
        functools.partial(expert_kernel, want_out, want_back),
        out_shape=tuple(outs),
        in_specs=[vmem] * len(args),
        out_specs=tuple([vmem] * len(outs)),
        scratch_shapes=sums,
        cost_estimate=pl.CostEstimate(
            flops=products * (3 + 6 * int(want_back)), bytes_accessed=8 << 20, transcendentals=0
        ),
        name="experts_back" if want_back else "experts",
    )(*args)


def spread_out(own):
    far = swap(own, 2)
    return (own, swap(own, 1), far, swap(far, 1))


def gather_weights(gate_w, up_w, down_w):
    own_pair = jnp.concatenate([gate_w, up_w], axis=1)
    return (spread_out(own_pair), spread_out(down_w))


def reduce_blocks(blocks):
    near = blocks[0] + swap(blocks[1], 1).astype(F32)
    far = blocks[2] + swap(blocks[3], 1).astype(F32)
    return near + swap(far.astype(BF16), 2).astype(F32)


def slot_tables(routing, me):
    count = routing.shape[0]
    member = jnp.any(routing[:, :, None] == jnp.arange(E, dtype=jnp.int32)[None, None, :], axis=1)
    index = jnp.arange(count, dtype=jnp.int32)
    before = (index[:, None] > index[None, :]).astype(BF16)
    rank = dot(before, member.astype(BF16))
    code = jnp.where(member, rank, -1.0).astype(BF16)
    slots = jnp.arange(E * ROOM, dtype=jnp.int32)
    widen = (slots[None, :] // ROOM == jnp.arange(E, dtype=jnp.int32)[:, None]).astype(BF16)
    wanted = (slots % ROOM) * WAYS + me
    pick = dot(code, widen) == wanted[None, :].astype(F32)
    return (member, pick, widen)


def attention_forward(hidden, gain, weights, rope):
    wq, wk, wv, wo = weights
    cosine, sine, allowed = rope
    normed, inverse = norm_forward(hidden, gain)
    normed_b = normed.astype(BF16)
    query = project_heads(normed_b, wq, cosine, sine, True)
    keys = project_heads(normed_b, wk, cosine, sine, True)
    values = project_heads(normed_b, wv, cosine, sine, False)
    mixed, lse = attend(query, keys, values, allowed)
    part = dot(mixed, wo)
    return part, (normed_b, inverse, query, keys, values, mixed, lse)


def attention_backward(d_middle_b, saved, weights, rope):
    wq, wk, wv, wo = weights
    cosine, sine, allowed = rope
    normed_b, inverse, query, keys, values, mixed, lse = saved
    count = normed_b.shape[0]
    d_mixed = dot(d_middle_b, wo, 1, 1).astype(BF16)
    d_query, d_keys, d_values = attend_back(query, keys, values, lse, allowed, d_mixed)
    d_query = unrotate(d_query, cosine, sine).reshape(count, -1).astype(BF16)
    d_keys = unrotate(d_keys, cosine, sine).reshape(count, -1).astype(BF16)
    d_values = d_values.reshape(count, -1).astype(BF16)
    part = dot(d_query, wq, 1, 1) + dot(d_keys, wk, 1, 1) + dot(d_values, wv, 1, 1)
    d_all = jnp.concatenate([d_query, d_keys, d_values], axis=1)
    return part, d_all


def router(middle, gain, w_router, tables):
    member, pick, widen = tables
    normed, inverse = norm_forward(middle, gain)
    moe_in = normed.astype(BF16)
    logits = jnp.where(member, dot(moe_in, w_router), NEGATIVE)
    top = jnp.max(logits, axis=-1, keepdims=True)
    expd = jnp.where(member, jnp.exp(logits - top), 0.0)
    gates = expd / jnp.sum(expd, axis=-1, keepdims=True)
    shares = jnp.where(pick, dot(gates.astype(BF16), widen), 0.0).astype(BF16)
    return moe_in, inverse, gates, shares


def gate_gradient(d_hidden_b, picked, gates, shares, widen):
    q = dot(
        dot(d_hidden_b, picked, 1, 1) * shares.astype(F32),
        widen.astype(F32),
        1,
        1,
        lax.Precision.HIGHEST,
    )
    return q - gates * jnp.sum(q, axis=-1, keepdims=True)


def columns(*parts):
    rows = parts[0].shape[0]
    width = sum(p.shape[1] for p in parts)
    pad = -width % 128
    parts = [p.astype(BF16) for p in parts]
    if pad:
        parts.append(jnp.zeros((rows, pad), BF16))
    return jnp.concatenate(parts, axis=1)


def per_device(
    hidden_in,
    cotangent,
    seq_lengths,
    routes,
    norm_attn,
    norm_moe,
    w_query,
    w_key,
    w_value,
    w_output,
    w_router,
    w_gate,
    w_up,
    w_down,
):
    count, width = hidden_in.shape
    me = lax.axis_index("tensor")
    rope = rope_tables(seq_lengths[0], count)
    expert_weights = [gather_weights(w_gate[l, 0], w_up[l, 0], w_down[l, 0]) for l in range(2)]
    tables = [slot_tables(routes[l], me) for l in range(2)]
    attn_weights = [(w_query[l], w_key[l], w_value[l], w_output[l]) for l in range(2)]
    slots = E * ROOM

    def middle_of(hidden, layer):
        part, saved = attention_forward(hidden, norm_attn[layer], attn_weights[layer], rope)
        return hidden + tensor_total(part), saved

    def moe_backward(layer, middle, inverse, moe_in, gates, d_log_part, back, d_hidden):
        pick = tables[layer][1].astype(BF16)
        payload = jnp.concatenate(
            [dot(pick, back), d_log_part, jnp.zeros((count, 128 - E), F32)], axis=1
        )
        summed = tensor_total(payload)
        d_logits = summed[:, width : width + E]
        router_f = w_router[layer].astype(F32)
        d_normed = summed[:, :width] + dot(d_logits, router_f, 1, 1, lax.Precision.HIGHEST)
        d_router = dot(moe_in, d_logits.astype(BF16), 0, 0)
        d_norm, d_gain = norm_backward(middle, inverse, norm_moe[layer], d_normed)
        return d_hidden + d_norm, d_gain, d_router

    def attn_backward(layer, hidden, saved, d_middle):
        d_middle_b = d_middle.astype(BF16)
        d_output_t = dot(d_middle_b, saved[5], 0, 0)
        part, d_all = attention_backward(d_middle_b, saved, attn_weights[layer], rope)
        d_in_w = dot(saved[0], d_all, 0, 0)
        d_norm, d_gain = norm_backward(
            hidden, saved[1], norm_attn[layer], tensor_total(part)
        )
        return d_middle + d_norm, d_gain, d_in_w, d_output_t

    middle0, saved0 = middle_of(hidden_in, 0)
    moe_in0, inverse0, gates0, shares0 = router(middle0, norm_moe[0], w_router[0], tables[0])
    send = dot(tables[0][1].astype(BF16), moe_in0, 0, 0).astype(BF16)
    received0 = exchange(send)
    (out,) = experts(received0, None, expert_weights[0], True)
    picked0 = exchange(out)
    hidden1 = middle0 + tensor_total(dot(shares0, picked0))

    middle1, saved1 = middle_of(hidden1, 1)
    moe_in1, inverse1, gates1, shares1 = router(middle1, norm_moe[1], w_router[1], tables[1])
    cot_b = cotangent.astype(BF16)
    send = dot(tables[1][1].astype(BF16), moe_in1, 0, 0).astype(BF16)
    d_send = dot(shares1, cot_b, 0, 0).astype(BF16)

    def couple(a, b):
        a, b = a.reshape(E, ROOM, width), b.reshape(E, ROOM, width)
        both = exchange(jnp.concatenate([a, b], axis=1).reshape(2 * slots, width))
        both = both.reshape(E, 2 * ROOM, width)
        return both[:, :ROOM].reshape(slots, width), both[:, ROOM:].reshape(slots, width)

    received1, d_received1 = couple(send, d_send)
    out, d_in, *expert_grads1 = experts(received1, d_received1, expert_weights[1], True)
    picked1, back1 = couple(out, d_in)
    d_log_part = gate_gradient(cot_b, picked1, gates1, shares1, tables[1][2])
    d_middle1, d_gain_two1, d_router1 = moe_backward(
        1, middle1, inverse1, moe_in1, gates1, d_log_part, back1, cotangent
    )
    output = middle1 + tensor_total(dot(shares1, picked1))
    d_hidden1, d_gain_one1, d_in_w1, d_output_t1 = attn_backward(1, hidden1, saved1, d_middle1)

    d_hidden1_b = d_hidden1.astype(BF16)
    d_send = dot(shares0, d_hidden1_b, 0, 0).astype(BF16)
    d_received0 = exchange(d_send)
    d_in, *expert_grads0 = experts(received0, d_received0, expert_weights[0], False)
    back0 = exchange(d_in)
    d_log_part = gate_gradient(d_hidden1_b, picked0, gates0, shares0, tables[0][2])
    d_middle0, d_gain_two0, d_router0 = moe_backward(
        0, middle0, inverse0, moe_in0, gates0, d_log_part, back0, d_hidden1
    )
    d_hidden0, d_gain_one0, d_in_w0, d_output_t0 = attn_backward(0, hidden_in, saved0, d_middle0)

    sums1 = dp_total(
        columns(d_in_w1, d_output_t1, d_router1, d_gain_one1[:, None], d_gain_two1[:, None])
    )
    early0 = dp_total(columns(d_output_t0, d_router0, d_gain_two0[:, None]))
    late0 = dp_total(columns(d_in_w0, d_gain_one0[:, None]))
    sums0 = jnp.concatenate(
        [late0[:, :512], early0[:, :288], late0[:, 512:513], early0[:, 288:289]], axis=1
    )
    both = jnp.stack([sums0, sums1[:, :802]])
    pair_grads = jnp.stack([reduce_blocks(g[:WAYS]) for g in (expert_grads0, expert_grads1)])
    down_grads = jnp.stack([reduce_blocks(g[WAYS:]) for g in (expert_grads0, expert_grads1)])
    return (
        output,
        d_hidden0,
        both[:, :, 800],
        both[:, :, 801],
        both[:, :, :256],
        both[:, :, 256:384],
        both[:, :, 384:512],
        jnp.swapaxes(both[:, :, 512:768], 1, 2),
        both[:, :, 768:800],
        pair_grads[:, None, :, :128],
        pair_grads[:, None, :, 128:],
        down_grads[:, None],
    )


def solution(mesh):
    in_specs = (
        P("dp", None),
        P("dp", None),
        P("dp", None),
        P(None, "dp", None),
        P(),
        P(),
        P(None, None, "tensor"),
        P(None, None, "tensor"),
        P(None, None, "tensor"),
        P(None, "tensor", None),
        P(),
        P(None, "dp", None, "tensor"),
        P(None, "dp", None, "tensor"),
        P(None, "dp", "tensor", None),
    )
    out_specs = (
        P("dp", None),
        P("dp", None),
        P(None, "dp"),
        P(None, "dp"),
        P(None, "dp", "tensor"),
        P(None, "dp", "tensor"),
        P(None, "dp", "tensor"),
        P(None, "tensor", "dp"),
        P(None, "dp", None),
        P(None, "dp", None, "tensor"),
        P(None, "dp", None, "tensor"),
        P(None, "dp", "tensor", None),
    )
    return jax.shard_map(
        per_device, mesh=mesh, in_specs=in_specs, out_specs=out_specs, check_vma=False
    )
```
